32 devices in a mesh: seq: 8 (over z, x), dp: 4 (over y, core).
Axes of the slice: x: 2, y: 2, z: 4, core: 2. Of those that a mesh axis runs over, the one named last changes fastest.
Arguments:
- inputs: bfloat16 [4, 1024, 8192], P('dp', 'seq'), may hold values from -8 to 8
- adapter_down_weight: bfloat16 [8192, 128], replicated, may hold values from -0.0625 to 0.0625
- adapter_up_weight: bfloat16 [384, 128], replicated, may hold values from -0.3125 to 0.3125
- query: bfloat16 [4, 1024, 128], P('dp', 'seq'), may hold values from -6 to 6
- key: bfloat16 [4, 1024, 128], P('dp', 'seq'), may hold values from -6 to 6
- value: bfloat16 [4, 1024, 128], P('dp', 'seq'), may hold values from -6 to 6
- output_gradient: bfloat16 [4, 1024, 128], P('dp', 'seq'), may hold values from -6 to 6
Outputs:
- query_grad: bfloat16 [4, 1024, 128], P('dp', 'seq')
- key_grad: bfloat16 [4, 1024, 128], P('dp', 'seq')
- value_grad: bfloat16 [4, 1024, 128], P('dp', 'seq')
- down_grad: float32 [8192, 128], P('dp')
- up_grad: float32 [384, 128], P('dp')
The draws below stay inside these ranges and needn't reach their ends.
All inputs are finite; a program needn't handle non-finite values.
Results may differ from the reference program's by a relative error of at most 0.0058.
Values sent between devices are 32-bit elements; how exact they have to be, the bound alone decides.
A program may use at most 64 MiB of HBM per device.

```python
import math
import jax
import jax.numpy as jnp
from jax import lax

MODEL_DIM = 8192
HEAD_SIZE = 128
LOCAL_HEADS = 1
ADAPTER_RANK = 128
TOK_DEV = 128
L = 1024
BATCH = 4


def spiked(result, stream_key, source, target, blocks, factor):
    def block_of(dim):
        return (jnp.arange(result.shape[dim]) // (result.shape[dim] // blocks)).reshape((-1,) + (1,) * (result.ndim - 1 - dim))

    first = jax.random.permutation(stream_key, blocks)[block_of(target)]
    other_side = (block_of(target) + blocks // 2) % blocks
    return jnp.where((block_of(source) == first) | (block_of(source) == other_side), factor * result, result)


def levels(key, extent, cuts, low, top_value):
    def one(axis_at, blocks):
        steps = jax.random.uniform(jax.random.fold_in(jax.random.fold_in(key, 6), axis_at), (blocks,), jnp.float32, low / len(cuts), top_value / len(cuts))
        return jnp.repeat(jnp.exp(steps), extent[axis_at] // blocks).reshape((-1,) + (1,) * (len(extent) - axis_at - 1))

    gain = one(*cuts[0])
    for cut in cuts[1:]:
        gain = gain * one(*cut)
    return gain


def bell_draw(key, dims, spread, limit, shards=(), kind=jnp.bfloat16):
    drawn = spread * jax.random.normal(key, dims, jnp.float32)
    if shards:
        drawn = drawn * levels(key, dims, shards, -0.22, 0.18)
    return jnp.clip(drawn, -limit, limit).astype(kind)


def heavy_noise(own_key, extent, spread, most, cuts, heavy, held_as=jnp.bfloat16):
    values = spread * jax.random.normal(own_key, extent, jnp.float32)
    if cuts:
        values = values * levels(own_key, extent, cuts, -0.22, 0.18)
    return jnp.clip(spiked(values, jax.random.fold_in(own_key, 3), *heavy), -most, most).astype(held_as)


def setup_inputs(seed: int = 0) -> dict:
    arg_keys = jax.random.split(jax.random.key(seed), 8)
    inputs = heavy_noise(arg_keys[0], (BATCH, L, MODEL_DIM), 1.0, 8.0, ((0, 4), (1, 8)), (0, 2, 4, 2.0))
    adapter_down_weight = bell_draw(arg_keys[1], (MODEL_DIM, ADAPTER_RANK), MODEL_DIM ** -0.5, 0.0625)
    adapter_up_weight = bell_draw(arg_keys[2], (3 * LOCAL_HEADS * HEAD_SIZE, ADAPTER_RANK), (3 * LOCAL_HEADS * HEAD_SIZE) ** -0.5, 0.3125)
    query = bell_draw(arg_keys[3], (BATCH, L, LOCAL_HEADS * HEAD_SIZE), 1.0, 6.0, ((0, 4), (1, 8)))
    key = bell_draw(arg_keys[4], (BATCH, L, LOCAL_HEADS * HEAD_SIZE), 1.0, 6.0, ((0, 4), (1, 8)))
    value = bell_draw(arg_keys[5], (BATCH, L, LOCAL_HEADS * HEAD_SIZE), 1.0, 6.0, ((0, 4), (1, 8)))
    output_gradient = bell_draw(arg_keys[6], (BATCH, L, LOCAL_HEADS * HEAD_SIZE), 1.0, 6.0, ((0, 4), (1, 8)))
    return {"inputs": inputs, "adapter_down_weight": adapter_down_weight, "adapter_up_weight": adapter_up_weight, "query": query, "key": key, "value": value, "output_gradient": output_gradient}


def hold(array):
    return lax.optimization_barrier(array.astype(jnp.bfloat16)).astype(jnp.float32)

def head_grads(query, key, value, output_gradient):
    blocks = L // TOK_DEV
    factor = 1.0 / math.sqrt(HEAD_SIZE * L)

    def split(array):
        return array.reshape(blocks, TOK_DEV, LOCAL_HEADS, HEAD_SIZE).astype(jnp.float32)
    queries = split(query)
    keys = split(key)
    values = split(value)
    grads_out = split(output_gradient)
    kv_state = jnp.einsum('nthi,nthj->nhij', keys, values)
    qg_state = jnp.einsum('nthi,nthj->nhij', queries, grads_out)
    zero_state = jnp.zeros((1, LOCAL_HEADS, HEAD_SIZE, HEAD_SIZE), jnp.float32)
    prefix = jnp.concatenate([zero_state, jnp.cumsum(kv_state, axis=0)[:-1]], axis=0)
    suffix = jnp.concatenate([jnp.cumsum(qg_state[::-1], axis=0)[:-1][::-1], zero_state], axis=0)
    prefix = hold(prefix)
    suffix = hold(suffix)
    rows_idx = lax.broadcasted_iota(jnp.int32, (TOK_DEV, TOK_DEV), 0)
    cols_idx = lax.broadcasted_iota(jnp.int32, (TOK_DEV, TOK_DEV), 1)
    causal = rows_idx >= cols_idx
    grad_scores = hold(jnp.where(causal, jnp.einsum('nthj,nshj->nhts', grads_out, values), 0.0))
    scores = hold(jnp.where(causal, jnp.einsum('nthi,nshi->nhts', queries, keys), 0.0))
    query_grad = jnp.einsum('nhts,nshi->nthi', grad_scores, keys) + jnp.einsum('nthj,nhij->nthi', grads_out, prefix)
    key_grad = jnp.einsum('nhts,nthi->nshi', grad_scores, queries) + jnp.einsum('nshj,nhij->nshi', values, suffix)
    value_grad = jnp.einsum('nhts,nthj->nshj', scores, grads_out) + jnp.einsum('nshi,nhij->nshj', keys, suffix)

    def finish(array):
        return (factor * array).reshape(L, LOCAL_HEADS * HEAD_SIZE).astype(jnp.bfloat16)
    return (finish(query_grad), finish(key_grad), finish(value_grad))

def reference(inputs, adapter_down_weight, adapter_up_weight, query, key, value, output_gradient):
    inverse = 1.0 / math.sqrt(BATCH * L)
    contract = (((0,), (0,)), ((), ()))

    def one_row(carry, items):
        input_rows, row_query, row_key, row_value, row_grad = items
        query_grad, key_grad, value_grad = head_grads(row_query, row_key, row_value, row_grad)
        gradient_list = jnp.concatenate([query_grad, key_grad, value_grad], axis=1)
        low_rank_state = jnp.dot(input_rows, adapter_down_weight, preferred_element_type=jnp.float32).astype(jnp.bfloat16)
        low_rank_gradient = jnp.dot(gradient_list, adapter_up_weight, preferred_element_type=jnp.float32).astype(jnp.bfloat16)
        down_sum = carry[0] + lax.dot_general(input_rows, low_rank_gradient, contract, preferred_element_type=jnp.float32)
        up_sum = carry[1] + lax.dot_general(gradient_list, low_rank_state, contract, preferred_element_type=jnp.float32)
        return ((down_sum, up_sum), (query_grad, key_grad, value_grad))
    start = (jnp.zeros((MODEL_DIM, ADAPTER_RANK), jnp.float32), jnp.zeros((3 * LOCAL_HEADS * HEAD_SIZE, ADAPTER_RANK), jnp.float32))
    sums, grads = lax.scan(one_row, start, (inputs, query, key, value, output_gradient))
    return (grads[0], grads[1], grads[2], sums[0] * inverse, sums[1] * inverse)
```

```python
import functools
import math

import jax
import jax.numpy as jnp
from jax import lax
from jax.experimental import pallas as pl
from jax.experimental.pallas import tpu as pltpu
from jax.sharding import PartitionSpec as P

HEAD_SIZE = 128
LOCAL_HEADS = 1


def entering(part, axis, combine, identity, reverse):
    count = lax.axis_size(axis)
    place = lax.axis_index(axis)
    ahead = count - 1 - place if reverse else place
    gathered = lax.all_gather(part, axis)
    state = jnp.zeros_like(part) + jnp.asarray(identity, part.dtype)

    def one(turn, state):
        source = count - 1 - turn if reverse else turn
        return combine(state, lax.dynamic_index_in_dim(gathered, source, 0, False))

    return lax.fori_loop(0, ahead, one, state)


def add_states(earlier, later):
    return earlier + later


def rounded_values(array):
    return array.astype(jnp.bfloat16)


def local(inputs, adapter_down_weight, adapter_up_weight, query, key, value, output_gradient):
    rows = query.shape[1]
    width = query.shape[2]
    seq_count = lax.axis_size("seq")
    dp_count = lax.axis_size("dp")
    length = rows * seq_count
    factor = 1.0 / math.sqrt(HEAD_SIZE * length)
    queries = query.reshape(rows, LOCAL_HEADS, HEAD_SIZE)
    keys = key.reshape(rows, LOCAL_HEADS, HEAD_SIZE)
    values = value.reshape(rows, LOCAL_HEADS, HEAD_SIZE)
    grads_out = output_gradient.reshape(rows, LOCAL_HEADS, HEAD_SIZE)
    kv_state = jnp.einsum("thi,thj->hij", keys, values, preferred_element_type=jnp.float32)
    qg_state = jnp.einsum("thi,thj->hij", queries, grads_out, preferred_element_type=jnp.float32)
    zeros = jnp.zeros_like(kv_state)
    prefix = entering(kv_state, "seq", add_states, zeros, False)
    suffix = entering(qg_state, "seq", add_states, zeros, True)
    prefix = rounded_values(prefix)
    suffix = rounded_values(suffix)
    rows_idx = lax.broadcasted_iota(jnp.int32, (rows, rows), 0)
    cols_idx = lax.broadcasted_iota(jnp.int32, (rows, rows), 1)
    causal = rows_idx >= cols_idx
    grad_scores = rounded_values(
        jnp.where(
            causal,
            jnp.einsum("thj,shj->hts", grads_out, values, preferred_element_type=jnp.float32),
            0.0,
        )
    )
    scores = rounded_values(
        jnp.where(
            causal,
            jnp.einsum("thi,shi->hts", queries, keys, preferred_element_type=jnp.float32),
            0.0,
        )
    )
    query_grad = jnp.einsum(
        "hts,shi->thi", grad_scores, keys, preferred_element_type=jnp.float32
    ) + jnp.einsum("thj,hij->thi", grads_out, prefix, preferred_element_type=jnp.float32)
    key_grad = jnp.einsum(
        "hts,thi->shi", grad_scores, queries, preferred_element_type=jnp.float32
    ) + jnp.einsum("shj,hij->shi", values, suffix, preferred_element_type=jnp.float32)
    value_grad = jnp.einsum(
        "hts,thj->shj", scores, grads_out, preferred_element_type=jnp.float32
    ) + jnp.einsum("shi,hij->shj", keys, suffix, preferred_element_type=jnp.float32)
    query_grad = rounded_values(factor * query_grad).reshape(rows, width)
    key_grad = rounded_values(factor * key_grad).reshape(rows, width)
    value_grad = rounded_values(factor * value_grad).reshape(rows, width)
    flattened = inputs.reshape(rows, inputs.shape[2])
    gradient_list = jnp.concatenate([query_grad, key_grad, value_grad], axis=1)
    low_rank_state = rounded_values(
        jnp.dot(flattened, adapter_down_weight, preferred_element_type=jnp.float32)
    )
    low_rank_gradient = rounded_values(
        jnp.dot(gradient_list, adapter_up_weight, preferred_element_type=jnp.float32)
    )
    inverse = 1.0 / math.sqrt(length * dp_count)
    contract = (((0,), (0,)), ((), ()))
    down_part = lax.psum_scatter(
        lax.dot_general(flattened, low_rank_gradient, contract, preferred_element_type=jnp.float32)
        * inverse,
        "dp",
        scatter_dimension=0,
        tiled=True,
    )
    up_term = (
        lax.dot_general(gradient_list, low_rank_state, contract, preferred_element_type=jnp.float32)
        * inverse
    )
    up_part = lax.psum_scatter(up_term, "dp", scatter_dimension=0, tiled=True)
    down_grad, up_grad = lax.psum((down_part, up_part), "seq")
    return (
        query_grad.reshape(1, rows, width),
        key_grad.reshape(1, rows, width),
        value_grad.reshape(1, rows, width),
        down_grad,
        up_grad,
    )


MESH = pl.DeviceIdType.MESH
CORES = 2
CHUNKS = 8


def fits(seq_count, dp_count):
    depth = seq_count // 2
    return dp_count == 2 * CORES and depth >= 2 and seq_count % 2 == 0 and depth & (depth - 1) == 0


def dot(a, b, da, db):
    return lax.dot_general(a, b, (((da,), (db,)), ((), ())), preferred_element_type=jnp.float32)


def fused_kernel(
    depth, factor, inverse,
    x_hbm, w_hbm, u_ref, q_ref, k_ref, v_ref, g_ref,
    qo_ref, ko_ref, vo_ref, down_ref, up_ref,
    x_ref, w_ref, xs_ref, xr_ref, xt_ref,
    st_ref, kvr_ref, qgr_ref, sxs_ref, sxr_ref,
    ls_ref, lr_ref, ups_ref, upr_ref, fg_ref,
    ys_ref, yr_ref, acc_ref, xrs_ref, zs_ref, zr_ref,
    load_sem, core_s, core_r, kv_s, kv_r, qg_s, qg_r, sx_s, sx_r,
    y_s, y_r, x_s, x_r, z_s, z_r, a_s, a_r,
):
    seq = lax.axis_index("seq")
    dp = lax.axis_index("dp")
    z, x = seq // 2, seq % 2
    y, c = dp // CORES, dp % CORES
    mate = {"seq": seq, "dp": y * CORES + (1 - c)}
    across = {"seq": seq, "dp": (1 - y) * CORES + c}
    beside = {"seq": z * 2 + (1 - x), "dp": dp}

    def along(other):
        return {"seq": other * 2 + x, "dp": dp}

    load_x = pltpu.make_async_copy(x_hbm, x_ref, load_sem.at[0])
    load_w = pltpu.make_async_copy(w_hbm, w_ref, load_sem.at[1])
    load_x.start()
    load_w.start()

    barrier = pltpu.get_barrier_semaphore()
    friends = [mate, across, beside] + [along(lax.rem(z + d, depth)) for d in range(1, depth)]
    for friend in friends:
        pl.semaphore_signal(barrier, inc=1, device_id=friend, device_id_type=MESH)

    rows = q_ref.shape[0]
    shard = down_ref.shape[0]
    ushard = up_ref.shape[0]
    width = q_ref.shape[1]
    q, k, v, g = q_ref[...], k_ref[...], v_ref[...], g_ref[...]
    st_ref[0] = dot(k, v, 0, 0)
    st_ref[1] = dot(q, g, 0, 0)
    pl.semaphore_wait(barrier, len(friends))

    def remote(src, dst, ssem, rsem, where):
        return pltpu.make_async_remote_copy(
            src_ref=src, dst_ref=dst, send_sem=ssem, recv_sem=rsem, device_id=where, device_id_type=MESH
        )

    ups, downs = [], []
    for d in range(1, depth):
        ups.append(remote(st_ref.at[0], kvr_ref.at[d - 1], kv_s.at[d - 1], kv_r.at[d - 1], along(lax.rem(z + d, depth))))
        downs.append(remote(st_ref.at[1], qgr_ref.at[d - 1], qg_s.at[d - 1], qg_r.at[d - 1], along(lax.rem(z - d + depth, depth))))
    for d in range(1, depth):
        pl.when(z + d < depth)(ups[d - 1].start)
        pl.when(z >= d)(downs[d - 1].start)

    load_x.wait()
    core_copies = []
    for part in range(2):
        cols = pl.ds(pl.multiple_of((part * CORES + 1 - c) * shard, 128), shard)
        xs_ref[part] = x_ref[:, cols].astype(jnp.float32)
        copy = remote(xs_ref.at[part], xr_ref.at[part], core_s.at[part], core_r.at[part], mate)
        copy.start()
        core_copies.append(copy)

    r_idx = lax.broadcasted_iota(jnp.int32, (rows, rows), 0)
    c_idx = lax.broadcasted_iota(jnp.int32, (rows, rows), 1)
    causal = r_idx >= c_idx
    gs = jnp.where(causal, dot(g, v, 1, 1), 0.0).astype(jnp.bfloat16)
    sc = jnp.where(causal, dot(q, k, 1, 1), 0.0).astype(jnp.bfloat16)
    q_in = dot(gs, k, 1, 0)
    k_in = dot(gs, q, 0, 0)
    v_in = dot(sc, g, 0, 0)

    for part in range(2):
        cols = pl.ds(pl.multiple_of((part * CORES + c) * shard, 128), shard)
        xt_ref[part, :, 0:rows] = x_ref[:, cols].T

    sxs_ref[...] = jnp.zeros_like(sxs_ref)
    for d in range(1, depth):
        @pl.when(z >= d)
        def _(d=d):
            ups[d - 1].wait_recv()
            sxs_ref[0] += kvr_ref[d - 1]

        @pl.when(z + d < depth)
        def _(d=d):
            downs[d - 1].wait_recv()
            sxs_ref[1] += qgr_ref[d - 1]

    prefix = sxs_ref[0]
    suffix = sxs_ref[1]

    @pl.when(x == 0)
    def _():
        sxs_ref[0] += st_ref[0]

    @pl.when(x == 1)
    def _():
        sxs_ref[1] += st_ref[1]

    swap = remote(sxs_ref, sxr_ref, sx_s, sx_r, beside)
    swap.start()

    load_w.wait()
    low = jnp.dot(x_ref[...], w_ref[...], preferred_element_type=jnp.float32).astype(jnp.bfloat16)
    for part in range(2):
        core_copies[part].wait_recv()
        xt_ref[part, :, rows:] = xr_ref[part].astype(jnp.bfloat16).T

    swap.wait_recv()
    prefix = (prefix + sxr_ref[0]).astype(jnp.bfloat16)
    suffix = (suffix + sxr_ref[1]).astype(jnp.bfloat16)
    q_grad = (factor * (q_in + dot(g, prefix, 1, 1))).astype(jnp.bfloat16)
    k_grad = (factor * (k_in + dot(v, suffix, 1, 1))).astype(jnp.bfloat16)
    v_grad = (factor * (v_in + dot(k, suffix, 1, 0))).astype(jnp.bfloat16)
    fg = jnp.concatenate([q_grad, k_grad, v_grad], axis=1)
    low_grad = dot(fg, u_ref[...], 1, 0).astype(jnp.bfloat16)
    ls_ref[...] = low_grad.astype(jnp.float32)
    low_copy = remote(ls_ref, lr_ref, core_s.at[2], core_r.at[2], mate)
    low_copy.start()
    qo_ref[...] = q_grad
    ko_ref[...] = k_grad
    vo_ref[...] = v_grad

    up_all = dot(fg, low, 0, 0)
    fg_ref[...] = up_all
    for part in range(2):
        rng = pl.ds(pl.multiple_of((part * CORES + 1 - c) * ushard, 8), ushard)
        ups_ref[part] = fg_ref[rng, :]
    up_copy = remote(ups_ref, upr_ref, core_s.at[3], core_r.at[3], mate)
    up_copy.start()

    low_copy.wait_recv()
    both = jnp.concatenate([low_grad, lr_ref[...].astype(jnp.bfloat16)], axis=0)

    size = shard // CHUNKS
    pieces = [(i * size, size) for i in range(CHUNKS)] + [(shard, ushard)]
    count = len(pieces)

    def partial(i, part):
        off, n = pieces[i]
        if off < shard:
            return jnp.dot(xt_ref[part, off : off + n, :], both, preferred_element_type=jnp.float32)
        mine = pl.ds(pl.multiple_of((part * CORES + c) * ushard, 8), ushard)
        return fg_ref[mine, :] + upr_ref[part]

    def half(i, which):
        off, n = pieces[i]
        return pl.ds(pl.multiple_of(off + which * (n // 2), 8), n // 2)

    def place(i, which):
        off, n = pieces[i]
        if off < shard:
            return down_ref.at[half(i, which), :]
        return up_ref.at[pl.ds(pl.multiple_of(which * (n // 2), 8), n // 2), :]

    y_copies, x_copies, a_copies = [], [], []
    z_copies = [[] for _ in range(depth.bit_length() - 1)]
    for i in range(count):
        off, n = pieces[i]
        if off >= shard:
            up_copy.wait_recv()
        ys_ref[off : off + n, :] = partial(i, 1 - y)
        copy = remote(ys_ref.at[off : off + n, :], yr_ref.at[off : off + n, :], y_s.at[i], y_r.at[i], across)
        copy.start()
        y_copies.append(copy)

    def x_stage(i):
        off, n = pieces[i]
        own = partial(i, y)
        y_copies[i].wait_recv()
        acc_ref[off : off + n, :] = own + yr_ref[off : off + n, :]
        h = n // 2
        short = pl.ds(off // 2, h)
        copy = remote(acc_ref.at[half(i, 1 - x), :], xrs_ref.at[short, :], x_s.at[i], x_r.at[i], beside)
        copy.start()
        x_copies.append(copy)

    def z_stage(i, level):
        off, n = pieces[i]
        h = n // 2
        short = slice(off // 2, off // 2 + h)
        if level == 0:
            x_copies[i].wait_recv()
            total = acc_ref[half(i, x), :] + xrs_ref[short, :]
        else:
            z_copies[level - 1][i].wait_recv()
            total = zs_ref[level - 1, short, :] + zr_ref[level - 1, short, :]
        if level < len(z_copies):
            zs_ref[level, short, :] = total
            bit = 1 << level
            other = z + bit - 2 * bit * ((z // bit) % 2)
            copy = remote(zs_ref.at[level, short, :], zr_ref.at[level, short, :], z_s.at[level, i], z_r.at[level, i], along(other))
            copy.start()
            z_copies[level].append(copy)
        else:
            spot = place(i, x)
            spot[...] = total * inverse
            copy = remote(spot, place(i, x), a_s.at[i], a_r.at[i], beside)
            copy.start()
            a_copies.append(copy)

    levels = len(z_copies) + 1
    for t in range(count + levels):
        if t < count:
            x_stage(t)
        for level in range(levels):
            i = t - 1 - level
            if 0 <= i < count:
                z_stage(i, level)

    for copy in a_copies:
        copy.wait_recv()
    for d in range(1, depth):
        pl.when(z + d < depth)(ups[d - 1].wait_send)
        pl.when(z >= d)(downs[d - 1].wait_send)
    for copy in core_copies + [swap, low_copy, up_copy] + y_copies + x_copies + sum(z_copies, []) + a_copies:
        copy.wait_send()


def fast(inputs, adapter_down_weight, adapter_up_weight, query, key, value, output_gradient):
    rows, width = query.shape[1:]
    model = inputs.shape[2]
    rank = adapter_down_weight.shape[1]
    features = adapter_up_weight.shape[0]
    seq_count = lax.axis_size("seq")
    dp_count = lax.axis_size("dp")
    length = rows * seq_count
    factor = 1.0 / math.sqrt(HEAD_SIZE * length)
    inverse = 1.0 / math.sqrt(length * dp_count)
    depth = seq_count // 2
    stages = depth.bit_length() - 1
    shard, ushard = model // dp_count, features // dp_count
    total = shard + ushard
    count = CHUNKS + 1
    f32, bf16 = jnp.float32, jnp.bfloat16
    dma = pltpu.SemaphoreType.DMA
    vmem = pl.BlockSpec(memory_space=pltpu.VMEM)
    hbm = pl.BlockSpec(memory_space=pl.ANY)
    out = pl.pallas_call(
        functools.partial(fused_kernel, depth, factor, inverse),
        out_shape=[jax.ShapeDtypeStruct((rows, width), bf16)] * 3
        + [jax.ShapeDtypeStruct((shard, rank), f32), jax.ShapeDtypeStruct((ushard, rank), f32)],
        in_specs=[hbm, hbm] + [vmem] * 5,
        out_specs=[vmem] * 5,
        scratch_shapes=[
            pltpu.VMEM((rows, model), bf16),
            pltpu.VMEM((model, rank), bf16),
            pltpu.VMEM((2, rows, shard), f32),
            pltpu.VMEM((2, rows, shard), f32),
            pltpu.VMEM((2, shard, 2 * rows), bf16),
            pltpu.VMEM((2, width, width), f32),
            pltpu.VMEM((depth - 1, width, width), f32),
            pltpu.VMEM((depth - 1, width, width), f32),
            pltpu.VMEM((2, width, width), f32),
            pltpu.VMEM((2, width, width), f32),
            pltpu.VMEM((rows, rank), f32),
            pltpu.VMEM((rows, rank), f32),
            pltpu.VMEM((2, ushard, rank), f32),
            pltpu.VMEM((2, ushard, rank), f32),
            pltpu.VMEM((features, rank), f32),
            pltpu.VMEM((total, rank), f32),
            pltpu.VMEM((total, rank), f32),
            pltpu.VMEM((total, rank), f32),
            pltpu.VMEM((total // 2, rank), f32),
            pltpu.VMEM((stages, total // 2, rank), f32),
            pltpu.VMEM((stages, total // 2, rank), f32),
            dma((2,)), dma((4,)), dma((4,)),
            dma((depth - 1,)), dma((depth - 1,)), dma((depth - 1,)), dma((depth - 1,)),
            dma, dma,
            dma((count,)), dma((count,)), dma((count,)), dma((count,)),
            dma((stages, count)), dma((stages, count)), dma((count,)), dma((count,)),
        ],
        compiler_params=pltpu.CompilerParams(collective_id=0, has_side_effects=True),
    )(
        inputs.reshape(rows, model), adapter_down_weight, adapter_up_weight,
        query.reshape(rows, width), key.reshape(rows, width),
        value.reshape(rows, width), output_gradient.reshape(rows, width),
    )
    return tuple(part.reshape(1, rows, width) for part in out[:3]) + tuple(out[3:])


def solution(mesh):
    fused = fits(mesh.shape["seq"], mesh.shape["dp"])
    chosen = fast if fused else local
    return jax.shard_map(
        chosen,
        mesh=mesh,
        in_specs=(
            P("dp", "seq", None),
            P(),
            P(),
            P("dp", "seq", None),
            P("dp", "seq", None),
            P("dp", "seq", None),
            P("dp", "seq", None),
        ),
        out_specs=(
            P("dp", "seq", None),
            P("dp", "seq", None),
            P("dp", "seq", None),
            P("dp", None),
            P("dp", None),
        ),
        check_vma=False,
    )
```

```python
import functools
import math

import jax
import jax.numpy as jnp
from jax import lax
from jax.experimental import pallas as pl
from jax.experimental.pallas import tpu as pltpu
from jax.sharding import PartitionSpec as P

HEAD_SIZE = 128
LOCAL_HEADS = 1


def entering(part, axis, combine, identity, reverse):
    count = lax.axis_size(axis)
    place = lax.axis_index(axis)
    ahead = count - 1 - place if reverse else place
    gathered = lax.all_gather(part, axis)
    state = jnp.zeros_like(part) + jnp.asarray(identity, part.dtype)

    def one(turn, state):
        source = count - 1 - turn if reverse else turn
        return combine(state, lax.dynamic_index_in_dim(gathered, source, 0, False))

    return lax.fori_loop(0, ahead, one, state)


def add_states(earlier, later):
    return earlier + later


def rounded_values(array):
    return array.astype(jnp.bfloat16)


def local(inputs, adapter_down_weight, adapter_up_weight, query, key, value, output_gradient):
    rows = query.shape[1]
    width = query.shape[2]
    seq_count = lax.axis_size("seq")
    dp_count = lax.axis_size("dp")
    length = rows * seq_count
    factor = 1.0 / math.sqrt(HEAD_SIZE * length)
    queries = query.reshape(rows, LOCAL_HEADS, HEAD_SIZE)
    keys = key.reshape(rows, LOCAL_HEADS, HEAD_SIZE)
    values = value.reshape(rows, LOCAL_HEADS, HEAD_SIZE)
    grads_out = output_gradient.reshape(rows, LOCAL_HEADS, HEAD_SIZE)
    kv_state = jnp.einsum("thi,thj->hij", keys, values, preferred_element_type=jnp.float32)
    qg_state = jnp.einsum("thi,thj->hij", queries, grads_out, preferred_element_type=jnp.float32)
    zeros = jnp.zeros_like(kv_state)
    prefix = entering(kv_state, "seq", add_states, zeros, False)
    suffix = entering(qg_state, "seq", add_states, zeros, True)
    prefix = rounded_values(prefix)
    suffix = rounded_values(suffix)
    rows_idx = lax.broadcasted_iota(jnp.int32, (rows, rows), 0)
    cols_idx = lax.broadcasted_iota(jnp.int32, (rows, rows), 1)
    causal = rows_idx >= cols_idx
    grad_scores = rounded_values(
        jnp.where(
            causal,
            jnp.einsum("thj,shj->hts", grads_out, values, preferred_element_type=jnp.float32),
            0.0,
        )
    )
    scores = rounded_values(
        jnp.where(
            causal,
            jnp.einsum("thi,shi->hts", queries, keys, preferred_element_type=jnp.float32),
            0.0,
        )
    )
    query_grad = jnp.einsum(
        "hts,shi->thi", grad_scores, keys, preferred_element_type=jnp.float32
    ) + jnp.einsum("thj,hij->thi", grads_out, prefix, preferred_element_type=jnp.float32)
    key_grad = jnp.einsum(
        "hts,thi->shi", grad_scores, queries, preferred_element_type=jnp.float32
    ) + jnp.einsum("shj,hij->shi", values, suffix, preferred_element_type=jnp.float32)
    value_grad = jnp.einsum(
        "hts,thj->shj", scores, grads_out, preferred_element_type=jnp.float32
    ) + jnp.einsum("shi,hij->shj", keys, suffix, preferred_element_type=jnp.float32)
    query_grad = rounded_values(factor * query_grad).reshape(rows, width)
    key_grad = rounded_values(factor * key_grad).reshape(rows, width)
    value_grad = rounded_values(factor * value_grad).reshape(rows, width)
    flattened = inputs.reshape(rows, inputs.shape[2])
    gradient_list = jnp.concatenate([query_grad, key_grad, value_grad], axis=1)
    low_rank_state = rounded_values(
        jnp.dot(flattened, adapter_down_weight, preferred_element_type=jnp.float32)
    )
    low_rank_gradient = rounded_values(
        jnp.dot(gradient_list, adapter_up_weight, preferred_element_type=jnp.float32)
    )
    inverse = 1.0 / math.sqrt(length * dp_count)
    contract = (((0,), (0,)), ((), ()))
    down_part = lax.psum_scatter(
        lax.dot_general(flattened, low_rank_gradient, contract, preferred_element_type=jnp.float32)
        * inverse,
        "dp",
        scatter_dimension=0,
        tiled=True,
    )
    up_term = (
        lax.dot_general(gradient_list, low_rank_state, contract, preferred_element_type=jnp.float32)
        * inverse
    )
    up_part = lax.psum_scatter(up_term, "dp", scatter_dimension=0, tiled=True)
    down_grad, up_grad = lax.psum((down_part, up_part), "seq")
    return (
        query_grad.reshape(1, rows, width),
        key_grad.reshape(1, rows, width),
        value_grad.reshape(1, rows, width),
        down_grad,
        up_grad,
    )


MESH = pl.DeviceIdType.MESH
CORES = 2
CHUNKS = 16
SKEW = 3


def fits(seq_count, dp_count):
    depth = seq_count // 2
    return dp_count == 2 * CORES and depth >= 2 and seq_count % 2 == 0 and depth & (depth - 1) == 0


def dot(a, b, da, db):
    return lax.dot_general(a, b, (((da,), (db,)), ((), ())), preferred_element_type=jnp.float32)


def fused_kernel(
    depth, factor, inverse,
    x_hbm, w_hbm, u_ref, q_ref, k_ref, v_ref, g_ref,
    qo_ref, ko_ref, vo_ref, down_ref, up_ref,
    x_ref, w_ref, xs_ref, xr_ref, xt_ref,
    st_ref, pair_ref, kvr_ref, qgr_ref, ox_ref, sxs_ref, sxr_ref,
    ls_ref, lr_ref, ups_ref, upr_ref, fg_ref,
    ys_ref, yr_ref, acc_ref, xrs_ref, zs_ref, zr_ref, us_ref, ur_ref,
    load_sem, core_s, core_r, kv_s, kv_r, qg_s, qg_r, sx_s, sx_r,
    y_s, y_r, x_s, x_r, z_s, z_r, b_s, b_r, a_s, a_r,
):
    seq = lax.axis_index("seq")
    dp = lax.axis_index("dp")
    z, x = seq // 2, seq % 2
    y, c = dp // CORES, dp % CORES
    mate = {"seq": seq, "dp": y * CORES + (1 - c)}
    across = {"seq": seq, "dp": (1 - y) * CORES + c}
    beside = {"seq": z * 2 + (1 - x), "dp": dp}

    def along(other):
        return {"seq": other * 2 + x, "dp": dp}

    load_x = pltpu.make_async_copy(x_hbm, x_ref, load_sem.at[0])
    load_w = pltpu.make_async_copy(w_hbm, w_ref, load_sem.at[1])
    load_x.start()
    load_w.start()

    barrier = pltpu.get_barrier_semaphore()
    friends = [mate, across, beside] + [along(lax.rem(z + d, depth)) for d in range(1, depth)]
    for friend in friends:
        pl.semaphore_signal(barrier, inc=1, device_id=friend, device_id_type=MESH)

    rows = q_ref.shape[0]
    shard = down_ref.shape[0]
    ushard = up_ref.shape[0]
    width = q_ref.shape[1]
    q, k, v, g = q_ref[...], k_ref[...], v_ref[...], g_ref[...]
    st_ref[0] = dot(k, v, 0, 0)
    st_ref[1] = dot(q, g, 0, 0)
    pl.semaphore_wait(barrier, len(friends))

    def remote(src, dst, ssem, rsem, where):
        return pltpu.make_async_remote_copy(
            src_ref=src, dst_ref=dst, send_sem=ssem, recv_sem=rsem, device_id=where, device_id_type=MESH
        )

    lead = width // 2
    first, second = slice(0, lead), slice(lead, width)
    other = remote(st_ref.at[:, second, :], ox_ref, sx_s.at[1], sx_r.at[1], beside)
    other.start()

    def scan(source, part, at):
        ups, downs = [], []
        for d in range(1, depth):
            slot = at * (depth - 1) + d - 1
            ups.append(remote(source.at[0, part, :], kvr_ref.at[d - 1, part, :], kv_s.at[slot], kv_r.at[slot], along(lax.rem(z + d, depth))))
            downs.append(remote(source.at[1, part, :], qgr_ref.at[d - 1, part, :], qg_s.at[slot], qg_r.at[slot], along(lax.rem(z - d + depth, depth))))
        for d in range(1, depth):
            pl.when(z + d < depth)(ups[d - 1].start)
            pl.when(z >= d)(downs[d - 1].start)
        return ups, downs

    def collect(ups, downs, part):
        sxs_ref[:, part, :] = jnp.zeros((2, lead, width), jnp.float32)
        for d in range(1, depth):
            @pl.when(z >= d)
            def _(d=d):
                ups[d - 1].wait_recv()
                sxs_ref[0, part, :] += kvr_ref[d - 1, part, :]

            @pl.when(z + d < depth)
            def _(d=d):
                downs[d - 1].wait_recv()
                sxs_ref[1, part, :] += qgr_ref[d - 1, part, :]

    scan_a = scan(st_ref, first, 0)

    load_x.wait()
    core_copies = []
    for part in range(2):
        cols = pl.ds(pl.multiple_of((part * CORES + 1 - c) * shard, 128), shard)
        xs_ref[part] = x_ref[:, cols].astype(jnp.float32)
        copy = remote(xs_ref.at[part], xr_ref.at[part], core_s.at[part], core_r.at[part], mate)
        copy.start()
        core_copies.append(copy)

    other.wait_recv()
    pair_ref[:, second, :] = st_ref[:, second, :] + ox_ref[...]
    scan_b = scan(pair_ref, second, 1)

    r_idx = lax.broadcasted_iota(jnp.int32, (rows, rows), 0)
    c_idx = lax.broadcasted_iota(jnp.int32, (rows, rows), 1)
    causal = r_idx >= c_idx
    gs = jnp.where(causal, dot(g, v, 1, 1), 0.0).astype(jnp.bfloat16)
    sc = jnp.where(causal, dot(q, k, 1, 1), 0.0).astype(jnp.bfloat16)
    q_in = dot(gs, k, 1, 0)
    k_in = dot(gs, q, 0, 0)
    v_in = dot(sc, g, 0, 0)

    for part in range(2):
        cols = pl.ds(pl.multiple_of((part * CORES + c) * shard, 128), shard)
        xt_ref[part, :, 0:rows] = x_ref[:, cols].T

    collect(*scan_a, first)
    lead_sum = sxs_ref[:, first, :]

    @pl.when(x == 0)
    def _():
        sxs_ref[0, first, :] += st_ref[0, first, :]

    @pl.when(x == 1)
    def _():
        sxs_ref[1, first, :] += st_ref[1, first, :]

    swap = remote(sxs_ref.at[:, first, :], sxr_ref, sx_s.at[0], sx_r.at[0], beside)
    swap.start()

    load_w.wait()
    low = jnp.dot(x_ref[...], w_ref[...], preferred_element_type=jnp.float32).astype(jnp.bfloat16)
    for part in range(2):
        core_copies[part].wait_recv()
        xt_ref[part, :, rows:] = xr_ref[part].astype(jnp.bfloat16).T

    collect(*scan_b, second)

    @pl.when(x == 1)
    def _():
        sxs_ref[0, second, :] += ox_ref[0]

    @pl.when(x == 0)
    def _():
        sxs_ref[1, second, :] += ox_ref[1]

    swap.wait_recv()
    states = jnp.concatenate([lead_sum + sxr_ref[...], sxs_ref[:, second, :]], axis=1).astype(jnp.bfloat16)
    prefix, suffix = states[0], states[1]
    q_grad = (factor * (q_in + dot(g, prefix, 1, 1))).astype(jnp.bfloat16)
    k_grad = (factor * (k_in + dot(v, suffix, 1, 1))).astype(jnp.bfloat16)
    v_grad = (factor * (v_in + dot(k, suffix, 1, 0))).astype(jnp.bfloat16)
    fg = jnp.concatenate([q_grad, k_grad, v_grad], axis=1)
    low_grad = dot(fg, u_ref[...], 1, 0).astype(jnp.bfloat16)
    ls_ref[...] = low_grad.astype(jnp.float32)
    low_copy = remote(ls_ref, lr_ref, core_s.at[2], core_r.at[2], mate)
    low_copy.start()
    qo_ref[...] = q_grad
    ko_ref[...] = k_grad
    vo_ref[...] = v_grad

    up_all = dot(fg, low, 0, 0)
    fg_ref[...] = up_all
    for part in range(2):
        rng = pl.ds(pl.multiple_of((part * CORES + 1 - c) * ushard, 8), ushard)
        ups_ref[part] = fg_ref[rng, :]
    up_copy = remote(ups_ref, upr_ref, core_s.at[3], core_r.at[3], mate)
    up_copy.start()

    low_copy.wait_recv()
    both = jnp.concatenate([low_grad, lr_ref[...].astype(jnp.bfloat16)], axis=0)

    size = shard // CHUNKS
    pieces = [(i * size, size) for i in range(CHUNKS)] + [(shard, ushard)]
    count = len(pieces)

    def partial(i, part):
        off, n = pieces[i]
        if off < shard:
            return jnp.dot(xt_ref[part, off : off + n, :], both, preferred_element_type=jnp.float32)
        mine = pl.ds(pl.multiple_of((part * CORES + c) * ushard, 8), ushard)
        return fg_ref[mine, :] + upr_ref[part]

    def half(i, which):
        off, n = pieces[i]
        return pl.ds(pl.multiple_of(off + which * (n // 2), 8), n // 2)

    def place(i, which, cuts):
        off, n = pieces[i]
        ref, base = (down_ref, off) if off < shard else (up_ref, 0)
        return ref.at[pl.ds(pl.multiple_of(base + which * (n // cuts), 8), n // cuts), :]

    y_copies, x_copies, a_copies = [], [], []
    b_copies = []
    top = depth.bit_length() - 1
    z_copies = [[] for _ in range(top)]
    b = z % 2

    def flip(level):
        bit = 1 << level
        return z + bit - 2 * bit * ((z // bit) % 2)

    for i in range(count):
        off, n = pieces[i]
        if off >= shard:
            up_copy.wait_recv()
        ys_ref[off : off + n, :] = partial(i, 1 - y)
        copy = remote(ys_ref.at[off : off + n, :], yr_ref.at[off : off + n, :], y_s.at[i], y_r.at[i], across)
        copy.start()
        y_copies.append(copy)

    def x_stage(i):
        off, n = pieces[i]
        own = partial(i, y)
        y_copies[i].wait_recv()
        acc_ref[off : off + n, :] = own + yr_ref[off : off + n, :]
        h = n // 2
        short = pl.ds(off // 2, h)
        copy = remote(acc_ref.at[half(i, 1 - x), :], xrs_ref.at[short, :], x_s.at[i], x_r.at[i], beside)
        copy.start()
        x_copies.append(copy)

    def z_stage(i, level):
        off, n = pieces[i]
        h, e = n // 2, n // 4
        if level == 0:
            x_copies[i].wait_recv()
            zs_ref[off // 2 : off // 2 + h, :] = acc_ref[half(i, x), :] + xrs_ref[off // 2 : off // 2 + h, :]
            away = pl.ds(pl.multiple_of(off // 2 + (1 - b) * e, 8), e)
            source, target = zs_ref.at[away, :], zr_ref.at[off // 4 : off // 4 + e, :]
        elif level <= top:
            z_copies[level - 1][i].wait_recv()
            short = slice(off // 4, off // 4 + e)
            if level == 1:
                kept = zs_ref[pl.ds(pl.multiple_of(off // 2 + b * e, 8), e), :] + zr_ref[short, :]
            else:
                kept = us_ref[level - 2, short, :] + ur_ref[level - 2, short, :]
            if level == top:
                spot = place(i, x * 2 + b, 4)
                spot[...] = kept * inverse
                copy = remote(spot, place(i, x * 2 + b, 4), b_s.at[i], b_r.at[i], along(flip(0)))
                copy.start()
                b_copies.append(copy)
                return
            us_ref[level - 1, short, :] = kept
            source, target = us_ref.at[level - 1, short, :], ur_ref.at[level - 1, short, :]
        else:
            b_copies[i].wait_recv()
            spot = place(i, x, 2)
            copy = remote(spot, place(i, x, 2), a_s.at[i], a_r.at[i], beside)
            copy.start()
            a_copies.append(copy)
            return
        copy = remote(source, target, z_s.at[level, i], z_r.at[level, i], along(flip(level)))
        copy.start()
        z_copies[level].append(copy)

    levels = top + 2
    for t in range(count + levels * SKEW):
        if t < count:
            x_stage(t)
        for level in range(levels):
            i = t - SKEW * (1 + level)
            if 0 <= i < count:
                z_stage(i, level)

    for copy in a_copies:
        copy.wait_recv()
    for ups, downs in (scan_a, scan_b):
        for d in range(1, depth):
            pl.when(z + d < depth)(ups[d - 1].wait_send)
            pl.when(z >= d)(downs[d - 1].wait_send)
    for copy in core_copies + [other, swap, low_copy, up_copy] + y_copies + x_copies + sum(z_copies, []) + b_copies + a_copies:
        copy.wait_send()


def write_out(*refs):
    copies = [pltpu.make_async_copy(refs[i], refs[5 + i], refs[10].at[i]) for i in range(5)]
    for copy in copies:
        copy.start()
    for copy in copies:
        copy.wait()


def fast(inputs, adapter_down_weight, adapter_up_weight, query, key, value, output_gradient):
    rows, width = query.shape[1:]
    model = inputs.shape[2]
    rank = adapter_down_weight.shape[1]
    features = adapter_up_weight.shape[0]
    seq_count = lax.axis_size("seq")
    dp_count = lax.axis_size("dp")
    length = rows * seq_count
    factor = 1.0 / math.sqrt(HEAD_SIZE * length)
    inverse = 1.0 / math.sqrt(length * dp_count)
    depth = seq_count // 2
    stages = depth.bit_length() - 1
    shard, ushard = model // dp_count, features // dp_count
    total = shard + ushard
    count = CHUNKS + 1
    f32, bf16 = jnp.float32, jnp.bfloat16
    dma = pltpu.SemaphoreType.DMA
    vmem = pl.BlockSpec(memory_space=pltpu.VMEM)
    hbm = pl.BlockSpec(memory_space=pl.ANY)
    shapes = [jax.ShapeDtypeStruct((rows, width), bf16)] * 3 + [
        jax.ShapeDtypeStruct((shard, rank), f32),
        jax.ShapeDtypeStruct((ushard, rank), f32),
    ]
    out = pl.pallas_call(
        functools.partial(fused_kernel, depth, factor, inverse),
        out_shape=shapes,
        in_specs=[hbm, hbm] + [vmem] * 5,
        out_specs=[vmem] * 5,
        scratch_shapes=[
            pltpu.VMEM((rows, model), bf16),
            pltpu.VMEM((model, rank), bf16),
            pltpu.VMEM((2, rows, shard), f32),
            pltpu.VMEM((2, rows, shard), f32),
            pltpu.VMEM((2, shard, 2 * rows), bf16),
            pltpu.VMEM((2, width, width), f32),
            pltpu.VMEM((2, width, width), f32),
            pltpu.VMEM((depth - 1, width, width), f32),
            pltpu.VMEM((depth - 1, width, width), f32),
            pltpu.VMEM((2, width // 2, width), f32),
            pltpu.VMEM((2, width, width), f32),
            pltpu.VMEM((2, width // 2, width), f32),
            pltpu.VMEM((rows, rank), f32),
            pltpu.VMEM((rows, rank), f32),
            pltpu.VMEM((2, ushard, rank), f32),
            pltpu.VMEM((2, ushard, rank), f32),
            pltpu.VMEM((features, rank), f32),
            pltpu.VMEM((total, rank), f32),
            pltpu.VMEM((total, rank), f32),
            pltpu.VMEM((total, rank), f32),
            pltpu.VMEM((total // 2, rank), f32),
            pltpu.VMEM((total // 2, rank), f32),
            pltpu.VMEM((total // 4, rank), f32),
            pltpu.VMEM((max(stages - 1, 1), total // 4, rank), f32),
            pltpu.VMEM((max(stages - 1, 1), total // 4, rank), f32),
            dma((2,)), dma((4,)), dma((4,)),
            dma((2 * depth - 2,)), dma((2 * depth - 2,)), dma((2 * depth - 2,)), dma((2 * depth - 2,)),
            dma((2,)), dma((2,)),
            dma((count,)), dma((count,)), dma((count,)), dma((count,)),
            dma((stages, count)), dma((stages, count)),
            dma((count,)), dma((count,)), dma((count,)), dma((count,)),
        ],
        compiler_params=pltpu.CompilerParams(
            collective_id=0, has_side_effects=True
        ),
    )(
        inputs.reshape(rows, model), adapter_down_weight, adapter_up_weight,
        query.reshape(rows, width), key.reshape(rows, width),
        value.reshape(rows, width), output_gradient.reshape(rows, width),
    )
    out = pl.pallas_call(
        write_out,
        out_shape=shapes,
        in_specs=[vmem] * 5,
        out_specs=[hbm] * 5,
        scratch_shapes=[dma((5,))],
    )(*out)
    return tuple(part.reshape(1, rows, width) for part in out[:3]) + tuple(out[3:])


def solution(mesh):
    fused = fits(mesh.shape["seq"], mesh.shape["dp"])
    chosen = fast if fused else local
    return jax.shard_map(
        chosen,
        mesh=mesh,
        in_specs=(
            P("dp", "seq", None),
            P(),
            P(),
            P("dp", "seq", None),
            P("dp", "seq", None),
            P("dp", "seq", None),
            P("dp", "seq", None),
        ),
        out_specs=(
            P("dp", "seq", None),
            P("dp", "seq", None),
            P("dp", "seq", None),
            P("dp", None),
            P("dp", None),
        ),
        check_vma=False,
    )
```

```python
import functools
import math

import jax
import jax.numpy as jnp
from jax import lax
from jax.experimental import pallas as pl
from jax.experimental.pallas import tpu as pltpu
from jax.sharding import PartitionSpec as P

HEAD_SIZE = 128
LOCAL_HEADS = 1


def entering(part, axis, combine, identity, reverse):
    count = lax.axis_size(axis)
    place = lax.axis_index(axis)
    ahead = count - 1 - place if reverse else place
    gathered = lax.all_gather(part, axis)
    state = jnp.zeros_like(part) + jnp.asarray(identity, part.dtype)

    def one(turn, state):
        source = count - 1 - turn if reverse else turn
        return combine(state, lax.dynamic_index_in_dim(gathered, source, 0, False))

    return lax.fori_loop(0, ahead, one, state)


def add_states(earlier, later):
    return earlier + later


def rounded_values(array):
    return array.astype(jnp.bfloat16)


def local(inputs, adapter_down_weight, adapter_up_weight, query, key, value, output_gradient):
    rows = query.shape[1]
    width = query.shape[2]
    seq_count = lax.axis_size("seq")
    dp_count = lax.axis_size("dp")
    length = rows * seq_count
    factor = 1.0 / math.sqrt(HEAD_SIZE * length)
    queries = query.reshape(rows, LOCAL_HEADS, HEAD_SIZE)
    keys = key.reshape(rows, LOCAL_HEADS, HEAD_SIZE)
    values = value.reshape(rows, LOCAL_HEADS, HEAD_SIZE)
    grads_out = output_gradient.reshape(rows, LOCAL_HEADS, HEAD_SIZE)
    kv_state = jnp.einsum("thi,thj->hij", keys, values, preferred_element_type=jnp.float32)
    qg_state = jnp.einsum("thi,thj->hij", queries, grads_out, preferred_element_type=jnp.float32)
    zeros = jnp.zeros_like(kv_state)
    prefix = entering(kv_state, "seq", add_states, zeros, False)
    suffix = entering(qg_state, "seq", add_states, zeros, True)
    prefix = rounded_values(prefix)
    suffix = rounded_values(suffix)
    rows_idx = lax.broadcasted_iota(jnp.int32, (rows, rows), 0)
    cols_idx = lax.broadcasted_iota(jnp.int32, (rows, rows), 1)
    causal = rows_idx >= cols_idx
    grad_scores = rounded_values(
        jnp.where(
            causal,
            jnp.einsum("thj,shj->hts", grads_out, values, preferred_element_type=jnp.float32),
            0.0,
        )
    )
    scores = rounded_values(
        jnp.where(
            causal,
            jnp.einsum("thi,shi->hts", queries, keys, preferred_element_type=jnp.float32),
            0.0,
        )
    )
    query_grad = jnp.einsum(
        "hts,shi->thi", grad_scores, keys, preferred_element_type=jnp.float32
    ) + jnp.einsum("thj,hij->thi", grads_out, prefix, preferred_element_type=jnp.float32)
    key_grad = jnp.einsum(
        "hts,thi->shi", grad_scores, queries, preferred_element_type=jnp.float32
    ) + jnp.einsum("shj,hij->shi", values, suffix, preferred_element_type=jnp.float32)
    value_grad = jnp.einsum(
        "hts,thj->shj", scores, grads_out, preferred_element_type=jnp.float32
    ) + jnp.einsum("shi,hij->shj", keys, suffix, preferred_element_type=jnp.float32)
    query_grad = rounded_values(factor * query_grad).reshape(rows, width)
    key_grad = rounded_values(factor * key_grad).reshape(rows, width)
    value_grad = rounded_values(factor * value_grad).reshape(rows, width)
    flattened = inputs.reshape(rows, inputs.shape[2])
    gradient_list = jnp.concatenate([query_grad, key_grad, value_grad], axis=1)
    low_rank_state = rounded_values(
        jnp.dot(flattened, adapter_down_weight, preferred_element_type=jnp.float32)
    )
    low_rank_gradient = rounded_values(
        jnp.dot(gradient_list, adapter_up_weight, preferred_element_type=jnp.float32)
    )
    inverse = 1.0 / math.sqrt(length * dp_count)
    contract = (((0,), (0,)), ((), ()))
    down_part = lax.psum_scatter(
        lax.dot_general(flattened, low_rank_gradient, contract, preferred_element_type=jnp.float32)
        * inverse,
        "dp",
        scatter_dimension=0,
        tiled=True,
    )
    up_term = (
        lax.dot_general(gradient_list, low_rank_state, contract, preferred_element_type=jnp.float32)
        * inverse
    )
    up_part = lax.psum_scatter(up_term, "dp", scatter_dimension=0, tiled=True)
    down_grad, up_grad = lax.psum((down_part, up_part), "seq")
    return (
        query_grad.reshape(1, rows, width),
        key_grad.reshape(1, rows, width),
        value_grad.reshape(1, rows, width),
        down_grad,
        up_grad,
    )


MESH = pl.DeviceIdType.MESH
CORES = 2
CHUNKS = 16
SKEW = 3


def fits(seq_count, dp_count):
    depth = seq_count // 2
    return dp_count == 2 * CORES and depth >= 2 and seq_count % 2 == 0 and depth & (depth - 1) == 0


def dot(a, b, da, db):
    return lax.dot_general(a, b, (((da,), (db,)), ((), ())), preferred_element_type=jnp.float32)


def fused_kernel(
    depth, factor, inverse,
    x_hbm, w_hbm, u_ref, q_ref, k_ref, v_ref, g_ref,
    qo_ref, ko_ref, vo_ref, down_ref, up_ref,
    x_ref, w_ref, xs_ref, xr_ref, xt_ref,
    st_ref, pair_ref, kvr_ref, qgr_ref, ox_ref, sxs_ref, sxr_ref,
    ls_ref, lr_ref, ups_ref, upr_ref, fg_ref,
    ys_ref, yr_ref, acc_ref, xrs_ref, zs_ref, zr_ref, us_ref, ur_ref,
    load_sem, core_s, core_r, kv_s, kv_r, qg_s, qg_r, sx_s, sx_r,
    y_s, y_r, x_s, x_r, z_s, z_r, b_s, b_r,
):
    seq = lax.axis_index("seq")
    dp = lax.axis_index("dp")
    z, x = seq // 2, seq % 2
    y, c = dp // CORES, dp % CORES
    mate = {"seq": seq, "dp": y * CORES + (1 - c)}
    across = {"seq": seq, "dp": (1 - y) * CORES + c}
    beside = {"seq": z * 2 + (1 - x), "dp": dp}

    corner = {"seq": (z + 1 - 2 * (z % 2)) * 2 + (1 - x), "dp": dp}

    def along(other):
        return {"seq": other * 2 + x, "dp": dp}

    load_x = pltpu.make_async_copy(x_hbm, x_ref, load_sem.at[0])
    load_w = pltpu.make_async_copy(w_hbm, w_ref, load_sem.at[1])
    load_x.start()
    load_w.start()

    barrier = pltpu.get_barrier_semaphore()
    friends = [mate, across, beside, corner] + [along(lax.rem(z + d, depth)) for d in range(1, depth)]
    for friend in friends:
        pl.semaphore_signal(barrier, inc=1, device_id=friend, device_id_type=MESH)

    rows = q_ref.shape[0]
    shard = down_ref.shape[0]
    ushard = up_ref.shape[0]
    width = q_ref.shape[1]
    q, k, v, g = q_ref[...], k_ref[...], v_ref[...], g_ref[...]
    st_ref[0] = dot(k, v, 0, 0)
    st_ref[1] = dot(q, g, 0, 0)
    pl.semaphore_wait(barrier, len(friends))

    def remote(src, dst, ssem, rsem, where):
        return pltpu.make_async_remote_copy(
            src_ref=src, dst_ref=dst, send_sem=ssem, recv_sem=rsem, device_id=where, device_id_type=MESH
        )

    lead = width // 2
    first, second = slice(0, lead), slice(lead, width)
    other = remote(st_ref.at[:, second, :], ox_ref, sx_s.at[1], sx_r.at[1], beside)
    other.start()

    def scan(source, part, at):
        ups, downs = [], []
        for d in range(1, depth):
            slot = at * (depth - 1) + d - 1
            ups.append(remote(source.at[0, part, :], kvr_ref.at[d - 1, part, :], kv_s.at[slot], kv_r.at[slot], along(lax.rem(z + d, depth))))
            downs.append(remote(source.at[1, part, :], qgr_ref.at[d - 1, part, :], qg_s.at[slot], qg_r.at[slot], along(lax.rem(z - d + depth, depth))))
        for d in range(1, depth):
            pl.when(z + d < depth)(ups[d - 1].start)
            pl.when(z >= d)(downs[d - 1].start)
        return ups, downs

    def collect(ups, downs, part):
        sxs_ref[:, part, :] = jnp.zeros((2, lead, width), jnp.float32)
        for d in range(1, depth):
            @pl.when(z >= d)
            def _(d=d):
                ups[d - 1].wait_recv()
                sxs_ref[0, part, :] += kvr_ref[d - 1, part, :]

            @pl.when(z + d < depth)
            def _(d=d):
                downs[d - 1].wait_recv()
                sxs_ref[1, part, :] += qgr_ref[d - 1, part, :]

    scan_a = scan(st_ref, first, 0)

    load_x.wait()
    core_copies = []
    for part in range(2):
        cols = pl.ds(pl.multiple_of((part * CORES + 1 - c) * shard, 128), shard)
        xs_ref[part] = x_ref[:, cols].astype(jnp.float32)
        copy = remote(xs_ref.at[part], xr_ref.at[part], core_s.at[part], core_r.at[part], mate)
        copy.start()
        core_copies.append(copy)

    other.wait_recv()
    pair_ref[:, second, :] = st_ref[:, second, :] + ox_ref[...]
    scan_b = scan(pair_ref, second, 1)

    r_idx = lax.broadcasted_iota(jnp.int32, (rows, rows), 0)
    c_idx = lax.broadcasted_iota(jnp.int32, (rows, rows), 1)
    causal = r_idx >= c_idx
    gs = jnp.where(causal, dot(g, v, 1, 1), 0.0).astype(jnp.bfloat16)
    sc = jnp.where(causal, dot(q, k, 1, 1), 0.0).astype(jnp.bfloat16)
    q_in = dot(gs, k, 1, 0)
    k_in = dot(gs, q, 0, 0)
    v_in = dot(sc, g, 0, 0)

    for part in range(2):
        cols = pl.ds(pl.multiple_of((part * CORES + c) * shard, 128), shard)
        xt_ref[part, :, 0:rows] = x_ref[:, cols].T

    collect(*scan_a, first)
    lead_sum = sxs_ref[:, first, :]

    @pl.when(x == 0)
    def _():
        sxs_ref[0, first, :] += st_ref[0, first, :]

    @pl.when(x == 1)
    def _():
        sxs_ref[1, first, :] += st_ref[1, first, :]

    swap = remote(sxs_ref.at[:, first, :], sxr_ref, sx_s.at[0], sx_r.at[0], beside)
    swap.start()

    for part in range(2):
        core_copies[part].wait_recv()
        xt_ref[part, :, rows:] = xr_ref[part].astype(jnp.bfloat16).T

    collect(*scan_b, second)

    @pl.when(x == 1)
    def _():
        sxs_ref[0, second, :] += ox_ref[0]

    @pl.when(x == 0)
    def _():
        sxs_ref[1, second, :] += ox_ref[1]

    swap.wait_recv()
    states = jnp.concatenate([lead_sum + sxr_ref[...], sxs_ref[:, second, :]], axis=1).astype(jnp.bfloat16)
    prefix, suffix = states[0], states[1]
    q_grad = (factor * (q_in + dot(g, prefix, 1, 1))).astype(jnp.bfloat16)
    k_grad = (factor * (k_in + dot(v, suffix, 1, 1))).astype(jnp.bfloat16)
    v_grad = (factor * (v_in + dot(k, suffix, 1, 0))).astype(jnp.bfloat16)
    fg = jnp.concatenate([q_grad, k_grad, v_grad], axis=1)
    low_grad = dot(fg, u_ref[...], 1, 0).astype(jnp.bfloat16)
    ls_ref[...] = low_grad.astype(jnp.float32)
    low_copy = remote(ls_ref, lr_ref, core_s.at[2], core_r.at[2], mate)
    low_copy.start()
    qo_ref[...] = q_grad
    ko_ref[...] = k_grad
    vo_ref[...] = v_grad

    low_copy.wait_recv()
    both = jnp.concatenate([low_grad, lr_ref[...].astype(jnp.bfloat16)], axis=0)

    size = shard // CHUNKS
    pieces = [(i * size, size) for i in range(CHUNKS)] + [(shard, ushard)]
    count = len(pieces)

    def partial(i, part):
        off, n = pieces[i]
        if off < shard:
            return jnp.dot(xt_ref[part, off : off + n, :], both, preferred_element_type=jnp.float32)
        mine = pl.ds(pl.multiple_of((part * CORES + c) * ushard, 8), ushard)
        return fg_ref[mine, :] + upr_ref[part]

    def half(i, which):
        off, n = pieces[i]
        return pl.ds(pl.multiple_of(off + which * (n // 2), 8), n // 2)

    def place(i, which, cuts):
        off, n = pieces[i]
        ref, base = (down_ref, off) if off < shard else (up_ref, 0)
        return ref.at[pl.ds(pl.multiple_of(base + which * (n // cuts), 8), n // cuts), :]

    y_copies, x_copies = [], []
    b_copies = []
    top = depth.bit_length() - 1
    z_copies = [[] for _ in range(top)]
    b = z % 2

    def flip(level):
        bit = 1 << level
        return z + bit - 2 * bit * ((z // bit) % 2)

    def y_stage(i):
        off, n = pieces[i]
        ys_ref[off : off + n, :] = partial(i, 1 - y)
        copy = remote(ys_ref.at[off : off + n, :], yr_ref.at[off : off + n, :], y_s.at[i], y_r.at[i], across)
        copy.start()
        y_copies.append(copy)

    for i in range(count - 1):
        y_stage(i)
    load_w.wait()
    low = jnp.dot(x_ref[...], w_ref[...], preferred_element_type=jnp.float32).astype(jnp.bfloat16)
    up_all = dot(fg, low, 0, 0)
    fg_ref[...] = up_all
    for part in range(2):
        rng = pl.ds(pl.multiple_of((part * CORES + 1 - c) * ushard, 8), ushard)
        ups_ref[part] = fg_ref[rng, :]
    up_copy = remote(ups_ref, upr_ref, core_s.at[3], core_r.at[3], mate)
    up_copy.start()

    up_copy.wait_recv()
    y_stage(count - 1)

    def x_stage(i):
        off, n = pieces[i]
        own = partial(i, y)
        y_copies[i].wait_recv()
        acc_ref[off : off + n, :] = own + yr_ref[off : off + n, :]
        h = n // 2
        short = pl.ds(off // 2, h)
        copy = remote(acc_ref.at[half(i, 1 - x), :], xrs_ref.at[short, :], x_s.at[i], x_r.at[i], beside)
        copy.start()
        x_copies.append(copy)

    def z_stage(i, level):
        off, n = pieces[i]
        h, e = n // 2, n // 4
        if level == 0:
            x_copies[i].wait_recv()
            zs_ref[off // 2 : off // 2 + h, :] = acc_ref[half(i, x), :] + xrs_ref[off // 2 : off // 2 + h, :]
            away = pl.ds(pl.multiple_of(off // 2 + (1 - b) * e, 8), e)
            source, target = zs_ref.at[away, :], zr_ref.at[off // 4 : off // 4 + e, :]
        else:
            z_copies[level - 1][i].wait_recv()
            short = slice(off // 4, off // 4 + e)
            if level == 1:
                kept = zs_ref[pl.ds(pl.multiple_of(off // 2 + b * e, 8), e), :] + zr_ref[short, :]
            else:
                kept = us_ref[level - 2, short, :] + ur_ref[level - 2, short, :]
            if level == top:
                spot = place(i, x * 2 + b, 4)
                spot[...] = kept * inverse
                for at, where in enumerate((beside, along(flip(0)), corner)):
                    copy = remote(spot, place(i, x * 2 + b, 4), b_s.at[at, i], b_r.at[at, i], where)
                    copy.start()
                    b_copies.append(copy)
                return
            us_ref[level - 1, short, :] = kept
            source, target = us_ref.at[level - 1, short, :], ur_ref.at[level - 1, short, :]
        copy = remote(source, target, z_s.at[level, i], z_r.at[level, i], along(flip(level)))
        copy.start()
        z_copies[level].append(copy)

    levels = top + 1
    for t in range(count + levels * SKEW):
        if t < count:
            x_stage(t)
        for level in range(levels):
            i = t - SKEW * (1 + level)
            if 0 <= i < count:
                z_stage(i, level)

    for copy in b_copies:
        copy.wait_recv()
    for ups, downs in (scan_a, scan_b):
        for d in range(1, depth):
            pl.when(z + d < depth)(ups[d - 1].wait_send)
            pl.when(z >= d)(downs[d - 1].wait_send)
    for copy in core_copies + [other, swap, low_copy, up_copy] + y_copies + x_copies + sum(z_copies, []) + b_copies:
        copy.wait_send()


def write_out(*refs):
    copies = [pltpu.make_async_copy(refs[i], refs[5 + i], refs[10].at[i]) for i in range(5)]
    for copy in copies:
        copy.start()
    for copy in copies:
        copy.wait()


def fast(inputs, adapter_down_weight, adapter_up_weight, query, key, value, output_gradient):
    rows, width = query.shape[1:]
    model = inputs.shape[2]
    rank = adapter_down_weight.shape[1]
    features = adapter_up_weight.shape[0]
    seq_count = lax.axis_size("seq")
    dp_count = lax.axis_size("dp")
    length = rows * seq_count
    factor = 1.0 / math.sqrt(HEAD_SIZE * length)
    inverse = 1.0 / math.sqrt(length * dp_count)
    depth = seq_count // 2
    stages = depth.bit_length() - 1
    shard, ushard = model // dp_count, features // dp_count
    total = shard + ushard
    count = CHUNKS + 1
    f32, bf16 = jnp.float32, jnp.bfloat16
    dma = pltpu.SemaphoreType.DMA
    vmem = pl.BlockSpec(memory_space=pltpu.VMEM)
    hbm = pl.BlockSpec(memory_space=pl.ANY)
    shapes = [jax.ShapeDtypeStruct((rows, width), bf16)] * 3 + [
        jax.ShapeDtypeStruct((shard, rank), f32),
        jax.ShapeDtypeStruct((ushard, rank), f32),
    ]
    out = pl.pallas_call(
        functools.partial(fused_kernel, depth, factor, inverse),
        out_shape=shapes,
        in_specs=[hbm, hbm] + [vmem] * 5,
        out_specs=[vmem] * 5,
        scratch_shapes=[
            pltpu.VMEM((rows, model), bf16),
            pltpu.VMEM((model, rank), bf16),
            pltpu.VMEM((2, rows, shard), f32),
            pltpu.VMEM((2, rows, shard), f32),
            pltpu.VMEM((2, shard, 2 * rows), bf16),
            pltpu.VMEM((2, width, width), f32),
            pltpu.VMEM((2, width, width), f32),
            pltpu.VMEM((depth - 1, width, width), f32),
            pltpu.VMEM((depth - 1, width, width), f32),
            pltpu.VMEM((2, width // 2, width), f32),
            pltpu.VMEM((2, width, width), f32),
            pltpu.VMEM((2, width // 2, width), f32),
            pltpu.VMEM((rows, rank), f32),
            pltpu.VMEM((rows, rank), f32),
            pltpu.VMEM((2, ushard, rank), f32),
            pltpu.VMEM((2, ushard, rank), f32),
            pltpu.VMEM((features, rank), f32),
            pltpu.VMEM((total, rank), f32),
            pltpu.VMEM((total, rank), f32),
            pltpu.VMEM((total, rank), f32),
            pltpu.VMEM((total // 2, rank), f32),
            pltpu.VMEM((total // 2, rank), f32),
            pltpu.VMEM((total // 4, rank), f32),
            pltpu.VMEM((max(stages - 1, 1), total // 4, rank), f32),
            pltpu.VMEM((max(stages - 1, 1), total // 4, rank), f32),
            dma((2,)), dma((4,)), dma((4,)),
            dma((2 * depth - 2,)), dma((2 * depth - 2,)), dma((2 * depth - 2,)), dma((2 * depth - 2,)),
            dma((2,)), dma((2,)),
            dma((count,)), dma((count,)), dma((count,)), dma((count,)),
            dma((stages, count)), dma((stages, count)),
            dma((3, count)), dma((3, count)),
        ],
        compiler_params=pltpu.CompilerParams(
            collective_id=0, has_side_effects=True
        ),
    )(
        inputs.reshape(rows, model), adapter_down_weight, adapter_up_weight,
        query.reshape(rows, width), key.reshape(rows, width),
        value.reshape(rows, width), output_gradient.reshape(rows, width),
    )
    out = pl.pallas_call(
        write_out,
        out_shape=shapes,
        in_specs=[vmem] * 5,
        out_specs=[hbm] * 5,
        scratch_shapes=[dma((5,))],
    )(*out)
    return tuple(part.reshape(1, rows, width) for part in out[:3]) + tuple(out[3:])


def solution(mesh):
    fused = fits(mesh.shape["seq"], mesh.shape["dp"])
    chosen = fast if fused else local
    return jax.shard_map(
        chosen,
        mesh=mesh,
        in_specs=(
            P("dp", "seq", None),
            P(),
            P(),
            P("dp", "seq", None),
            P("dp", "seq", None),
            P("dp", "seq", None),
            P("dp", "seq", None),
        ),
        out_specs=(
            P("dp", "seq", None),
            P("dp", "seq", None),
            P("dp", "seq", None),
            P("dp", None),
            P("dp", None),
        ),
        check_vma=False,
    )
```

```python
import functools
import math

import jax
import jax.numpy as jnp
from jax import lax
from jax.experimental import pallas as pl
from jax.experimental.pallas import tpu as pltpu
from jax.sharding import PartitionSpec as P

HEAD_SIZE = 128
LOCAL_HEADS = 1


def entering(part, axis, combine, identity, reverse):
    count = lax.axis_size(axis)
    place = lax.axis_index(axis)
    ahead = count - 1 - place if reverse else place
    gathered = lax.all_gather(part, axis)
    state = jnp.zeros_like(part) + jnp.asarray(identity, part.dtype)

    def one(turn, state):
        source = count - 1 - turn if reverse else turn
        return combine(state, lax.dynamic_index_in_dim(gathered, source, 0, False))

    return lax.fori_loop(0, ahead, one, state)


def add_states(earlier, later):
    return earlier + later


def rounded_values(array):
    return array.astype(jnp.bfloat16)


def local(inputs, adapter_down_weight, adapter_up_weight, query, key, value, output_gradient):
    rows = query.shape[1]
    width = query.shape[2]
    seq_count = lax.axis_size("seq")
    dp_count = lax.axis_size("dp")
    length = rows * seq_count
    factor = 1.0 / math.sqrt(HEAD_SIZE * length)
    queries = query.reshape(rows, LOCAL_HEADS, HEAD_SIZE)
    keys = key.reshape(rows, LOCAL_HEADS, HEAD_SIZE)
    values = value.reshape(rows, LOCAL_HEADS, HEAD_SIZE)
    grads_out = output_gradient.reshape(rows, LOCAL_HEADS, HEAD_SIZE)
    kv_state = jnp.einsum("thi,thj->hij", keys, values, preferred_element_type=jnp.float32)
    qg_state = jnp.einsum("thi,thj->hij", queries, grads_out, preferred_element_type=jnp.float32)
    zeros = jnp.zeros_like(kv_state)
    prefix = entering(kv_state, "seq", add_states, zeros, False)
    suffix = entering(qg_state, "seq", add_states, zeros, True)
    prefix = rounded_values(prefix)
    suffix = rounded_values(suffix)
    rows_idx = lax.broadcasted_iota(jnp.int32, (rows, rows), 0)
    cols_idx = lax.broadcasted_iota(jnp.int32, (rows, rows), 1)
    causal = rows_idx >= cols_idx
    grad_scores = rounded_values(
        jnp.where(
            causal,
            jnp.einsum("thj,shj->hts", grads_out, values, preferred_element_type=jnp.float32),
            0.0,
        )
    )
    scores = rounded_values(
        jnp.where(
            causal,
            jnp.einsum("thi,shi->hts", queries, keys, preferred_element_type=jnp.float32),
            0.0,
        )
    )
    query_grad = jnp.einsum(
        "hts,shi->thi", grad_scores, keys, preferred_element_type=jnp.float32
    ) + jnp.einsum("thj,hij->thi", grads_out, prefix, preferred_element_type=jnp.float32)
    key_grad = jnp.einsum(
        "hts,thi->shi", grad_scores, queries, preferred_element_type=jnp.float32
    ) + jnp.einsum("shj,hij->shi", values, suffix, preferred_element_type=jnp.float32)
    value_grad = jnp.einsum(
        "hts,thj->shj", scores, grads_out, preferred_element_type=jnp.float32
    ) + jnp.einsum("shi,hij->shj", keys, suffix, preferred_element_type=jnp.float32)
    query_grad = rounded_values(factor * query_grad).reshape(rows, width)
    key_grad = rounded_values(factor * key_grad).reshape(rows, width)
    value_grad = rounded_values(factor * value_grad).reshape(rows, width)
    flattened = inputs.reshape(rows, inputs.shape[2])
    gradient_list = jnp.concatenate([query_grad, key_grad, value_grad], axis=1)
    low_rank_state = rounded_values(
        jnp.dot(flattened, adapter_down_weight, preferred_element_type=jnp.float32)
    )
    low_rank_gradient = rounded_values(
        jnp.dot(gradient_list, adapter_up_weight, preferred_element_type=jnp.float32)
    )
    inverse = 1.0 / math.sqrt(length * dp_count)
    contract = (((0,), (0,)), ((), ()))
    down_part = lax.psum_scatter(
        lax.dot_general(flattened, low_rank_gradient, contract, preferred_element_type=jnp.float32)
        * inverse,
        "dp",
        scatter_dimension=0,
        tiled=True,
    )
    up_term = (
        lax.dot_general(gradient_list, low_rank_state, contract, preferred_element_type=jnp.float32)
        * inverse
    )
    up_part = lax.psum_scatter(up_term, "dp", scatter_dimension=0, tiled=True)
    down_grad, up_grad = lax.psum((down_part, up_part), "seq")
    return (
        query_grad.reshape(1, rows, width),
        key_grad.reshape(1, rows, width),
        value_grad.reshape(1, rows, width),
        down_grad,
        up_grad,
    )


MESH = pl.DeviceIdType.MESH
CORES = 2
CHUNKS = 16
SKEW = 3


def fits(seq_count, dp_count):
    depth = seq_count // 2
    return dp_count == 2 * CORES and depth >= 2 and seq_count % 2 == 0 and depth & (depth - 1) == 0


def dot(a, b, da, db):
    return lax.dot_general(a, b, (((da,), (db,)), ((), ())), preferred_element_type=jnp.float32)


def fused_kernel(
    depth, factor, inverse,
    x_hbm, w_hbm, u_ref, q_ref, k_ref, v_ref, g_ref,
    qo_ref, ko_ref, vo_ref, down_ref, up_ref,
    x_ref, w_ref, xs_ref, xr_ref, xt_ref,
    st_ref, pair_ref, kvr_ref, qgr_ref, ox_ref, sxs_ref, sxr_ref,
    ls_ref, lr_ref, ups_ref, upr_ref, fg_ref,
    ys_ref, yr_ref, acc_ref, xrs_ref, zs_ref, zr_ref, us_ref, ur_ref,
    load_sem, core_s, core_r, kv_s, kv_r, qg_s, qg_r, sx_s, sx_r,
    y_s, y_r, x_s, x_r, z_s, z_r, b_s, b_r, a_s, a_r,
):
    seq = lax.axis_index("seq")
    dp = lax.axis_index("dp")
    z, x = seq // 2, seq % 2
    y, c = dp // CORES, dp % CORES
    mate = {"seq": seq, "dp": y * CORES + (1 - c)}
    across = {"seq": seq, "dp": (1 - y) * CORES + c}
    beside = {"seq": z * 2 + (1 - x), "dp": dp}

    def along(other):
        return {"seq": other * 2 + x, "dp": dp}

    load_x = pltpu.make_async_copy(x_hbm, x_ref, load_sem.at[0])
    load_w = pltpu.make_async_copy(w_hbm, w_ref, load_sem.at[1])
    load_x.start()
    load_w.start()

    barrier = pltpu.get_barrier_semaphore()
    friends = [mate, across, beside] + [along(lax.rem(z + d, depth)) for d in range(1, depth)]
    for friend in friends:
        pl.semaphore_signal(barrier, inc=1, device_id=friend, device_id_type=MESH)

    rows = q_ref.shape[0]
    shard = down_ref.shape[0]
    ushard = up_ref.shape[0]
    width = q_ref.shape[1]
    q, k, v, g = q_ref[...], k_ref[...], v_ref[...], g_ref[...]
    st_ref[0] = dot(k, v, 0, 0)
    st_ref[1] = dot(q, g, 0, 0)
    pl.semaphore_wait(barrier, len(friends))

    def remote(src, dst, ssem, rsem, where):
        return pltpu.make_async_remote_copy(
            src_ref=src, dst_ref=dst, send_sem=ssem, recv_sem=rsem, device_id=where, device_id_type=MESH
        )

    lead = width // 2
    first, second = slice(0, lead), slice(lead, width)
    other = remote(st_ref.at[:, second, :], ox_ref, sx_s.at[1], sx_r.at[1], beside)
    other.start()

    def scan(source, part, at):
        ups, downs = [], []
        for d in range(1, depth):
            slot = at * (depth - 1) + d - 1
            ups.append(remote(source.at[0, part, :], kvr_ref.at[d - 1, part, :], kv_s.at[slot], kv_r.at[slot], along(lax.rem(z + d, depth))))
            downs.append(remote(source.at[1, part, :], qgr_ref.at[d - 1, part, :], qg_s.at[slot], qg_r.at[slot], along(lax.rem(z - d + depth, depth))))
        for d in range(1, depth):
            pl.when(z + d < depth)(ups[d - 1].start)
            pl.when(z >= d)(downs[d - 1].start)
        return ups, downs

    def collect(ups, downs, part):
        sxs_ref[:, part, :] = jnp.zeros((2, lead, width), jnp.float32)
        for d in range(1, depth):
            @pl.when(z >= d)
            def _(d=d):
                ups[d - 1].wait_recv()
                sxs_ref[0, part, :] += kvr_ref[d - 1, part, :]

            @pl.when(z + d < depth)
            def _(d=d):
                downs[d - 1].wait_recv()
                sxs_ref[1, part, :] += qgr_ref[d - 1, part, :]

    scan_a = scan(st_ref, first, 0)

    load_x.wait()
    core_copies = []
    for part in range(2):
        cols = pl.ds(pl.multiple_of((part * CORES + 1 - c) * shard, 128), shard)
        xs_ref[part] = x_ref[:, cols].astype(jnp.float32)
        copy = remote(xs_ref.at[part], xr_ref.at[part], core_s.at[part], core_r.at[part], mate)
        copy.start()
        core_copies.append(copy)

    other.wait_recv()
    pair_ref[:, second, :] = st_ref[:, second, :] + ox_ref[...]
    scan_b = scan(pair_ref, second, 1)

    r_idx = lax.broadcasted_iota(jnp.int32, (rows, rows), 0)
    c_idx = lax.broadcasted_iota(jnp.int32, (rows, rows), 1)
    causal = r_idx >= c_idx
    gs = jnp.where(causal, dot(g, v, 1, 1), 0.0).astype(jnp.bfloat16)
    sc = jnp.where(causal, dot(q, k, 1, 1), 0.0).astype(jnp.bfloat16)
    q_in = dot(gs, k, 1, 0)
    k_in = dot(gs, q, 0, 0)
    v_in = dot(sc, g, 0, 0)

    for part in range(2):
        cols = pl.ds(pl.multiple_of((part * CORES + c) * shard, 128), shard)
        xt_ref[part, :, 0:rows] = x_ref[:, cols].T

    collect(*scan_a, first)
    lead_sum = sxs_ref[:, first, :]

    @pl.when(x == 0)
    def _():
        sxs_ref[0, first, :] += st_ref[0, first, :]

    @pl.when(x == 1)
    def _():
        sxs_ref[1, first, :] += st_ref[1, first, :]

    swap = remote(sxs_ref.at[:, first, :], sxr_ref, sx_s.at[0], sx_r.at[0], beside)
    swap.start()

    for part in range(2):
        core_copies[part].wait_recv()
        xt_ref[part, :, rows:] = xr_ref[part].astype(jnp.bfloat16).T

    collect(*scan_b, second)

    @pl.when(x == 1)
    def _():
        sxs_ref[0, second, :] += ox_ref[0]

    @pl.when(x == 0)
    def _():
        sxs_ref[1, second, :] += ox_ref[1]

    swap.wait_recv()
    states = jnp.concatenate([lead_sum + sxr_ref[...], sxs_ref[:, second, :]], axis=1).astype(jnp.bfloat16)
    prefix, suffix = states[0], states[1]
    q_grad = (factor * (q_in + dot(g, prefix, 1, 1))).astype(jnp.bfloat16)
    k_grad = (factor * (k_in + dot(v, suffix, 1, 1))).astype(jnp.bfloat16)
    v_grad = (factor * (v_in + dot(k, suffix, 1, 0))).astype(jnp.bfloat16)
    fg = jnp.concatenate([q_grad, k_grad, v_grad], axis=1)
    low_grad = dot(fg, u_ref[...], 1, 0).astype(jnp.bfloat16)
    ls_ref[...] = low_grad.astype(jnp.float32)
    low_copy = remote(ls_ref, lr_ref, core_s.at[2], core_r.at[2], mate)
    low_copy.start()
    qo_ref[...] = q_grad
    ko_ref[...] = k_grad
    vo_ref[...] = v_grad

    low_copy.wait_recv()
    both = jnp.concatenate([low_grad, lr_ref[...].astype(jnp.bfloat16)], axis=0)

    size = shard // CHUNKS
    pieces = [(i * size, size) for i in range(CHUNKS)] + [(shard, ushard)]
    count = len(pieces)

    def partial(i, part):
        off, n = pieces[i]
        if off < shard:
            return jnp.dot(xt_ref[part, off : off + n, :], both, preferred_element_type=jnp.float32)
        mine = pl.ds(pl.multiple_of((part * CORES + c) * ushard, 8), ushard)
        return fg_ref[mine, :] + upr_ref[part]

    def half(i, which):
        off, n = pieces[i]
        return pl.ds(pl.multiple_of(off + which * (n // 2), 8), n // 2)

    def place(i, which, cuts):
        off, n = pieces[i]
        ref, base = (down_ref, off) if off < shard else (up_ref, 0)
        return ref.at[pl.ds(pl.multiple_of(base + which * (n // cuts), 8), n // cuts), :]

    y_copies, x_copies, a_copies = [], [], []
    b_copies = []
    top = depth.bit_length() - 1
    z_copies = [[] for _ in range(top)]
    b = z % 2

    def flip(level):
        bit = 1 << level
        return z + bit - 2 * bit * ((z // bit) % 2)

    def y_stage(i):
        off, n = pieces[i]
        ys_ref[off : off + n, :] = partial(i, 1 - y)
        copy = remote(ys_ref.at[off : off + n, :], yr_ref.at[off : off + n, :], y_s.at[i], y_r.at[i], across)
        copy.start()
        y_copies.append(copy)

    for i in range(count - 1):
        y_stage(i)
    load_w.wait()
    low = jnp.dot(x_ref[...], w_ref[...], preferred_element_type=jnp.float32).astype(jnp.bfloat16)
    up_all = dot(fg, low, 0, 0)
    fg_ref[...] = up_all
    for part in range(2):
        rng = pl.ds(pl.multiple_of((part * CORES + 1 - c) * ushard, 8), ushard)
        ups_ref[part] = fg_ref[rng, :]
    up_copy = remote(ups_ref, upr_ref, core_s.at[3], core_r.at[3], mate)
    up_copy.start()

    up_copy.wait_recv()
    y_stage(count - 1)

    def x_stage(i):
        off, n = pieces[i]
        own = partial(i, y)
        y_copies[i].wait_recv()
        acc_ref[off : off + n, :] = own + yr_ref[off : off + n, :]
        h = n // 2
        short = pl.ds(off // 2, h)
        copy = remote(acc_ref.at[half(i, 1 - x), :], xrs_ref.at[short, :], x_s.at[i], x_r.at[i], beside)
        copy.start()
        x_copies.append(copy)

    def z_stage(i, level):
        off, n = pieces[i]
        h, e = n // 2, n // 4
        if level == 0:
            x_copies[i].wait_recv()
            zs_ref[off // 2 : off // 2 + h, :] = acc_ref[half(i, x), :] + xrs_ref[off // 2 : off // 2 + h, :]
            away = pl.ds(pl.multiple_of(off // 2 + (1 - b) * e, 8), e)
            source, target = zs_ref.at[away, :], zr_ref.at[off // 4 : off // 4 + e, :]
        elif level <= top:
            z_copies[level - 1][i].wait_recv()
            short = slice(off // 4, off // 4 + e)
            if level == 1:
                kept = zs_ref[pl.ds(pl.multiple_of(off // 2 + b * e, 8), e), :] + zr_ref[short, :]
            else:
                kept = us_ref[level - 2, short, :] + ur_ref[level - 2, short, :]
            if level == top:
                spot = place(i, x * 2 + b, 4)
                spot[...] = kept * inverse
                copy = remote(spot, place(i, x * 2 + b, 4), b_s.at[i], b_r.at[i], along(flip(0)))
                copy.start()
                b_copies.append(copy)
                return
            us_ref[level - 1, short, :] = kept
            source, target = us_ref.at[level - 1, short, :], ur_ref.at[level - 1, short, :]
        else:
            b_copies[i].wait_recv()
            spot = place(i, x, 2)
            copy = remote(spot, place(i, x, 2), a_s.at[i], a_r.at[i], beside)
            copy.start()
            a_copies.append(copy)
            return
        copy = remote(source, target, z_s.at[level, i], z_r.at[level, i], along(flip(level)))
        copy.start()
        z_copies[level].append(copy)

    levels = top + 2
    for t in range(count + levels * SKEW):
        if t < count:
            x_stage(t)
        for level in range(levels):
            i = t - SKEW * (1 + level)
            if 0 <= i < count:
                z_stage(i, level)

    for copy in a_copies:
        copy.wait_recv()
    for ups, downs in (scan_a, scan_b):
        for d in range(1, depth):
            pl.when(z + d < depth)(ups[d - 1].wait_send)
            pl.when(z >= d)(downs[d - 1].wait_send)
    for copy in core_copies + [other, swap, low_copy, up_copy] + y_copies + x_copies + sum(z_copies, []) + b_copies + a_copies:
        copy.wait_send()


def write_out(*refs):
    copies = [pltpu.make_async_copy(refs[i], refs[5 + i], refs[10].at[i]) for i in range(5)]
    for copy in copies:
        copy.start()
    for copy in copies:
        copy.wait()


def fast(inputs, adapter_down_weight, adapter_up_weight, query, key, value, output_gradient):
    rows, width = query.shape[1:]
    model = inputs.shape[2]
    rank = adapter_down_weight.shape[1]
    features = adapter_up_weight.shape[0]
    seq_count = lax.axis_size("seq")
    dp_count = lax.axis_size("dp")
    length = rows * seq_count
    factor = 1.0 / math.sqrt(HEAD_SIZE * length)
    inverse = 1.0 / math.sqrt(length * dp_count)
    depth = seq_count // 2
    stages = depth.bit_length() - 1
    shard, ushard = model // dp_count, features // dp_count
    total = shard + ushard
    count = CHUNKS + 1
    f32, bf16 = jnp.float32, jnp.bfloat16
    dma = pltpu.SemaphoreType.DMA
    vmem = pl.BlockSpec(memory_space=pltpu.VMEM)
    hbm = pl.BlockSpec(memory_space=pl.ANY)
    shapes = [jax.ShapeDtypeStruct((rows, width), bf16)] * 3 + [
        jax.ShapeDtypeStruct((shard, rank), f32),
        jax.ShapeDtypeStruct((ushard, rank), f32),
    ]
    out = pl.pallas_call(
        functools.partial(fused_kernel, depth, factor, inverse),
        out_shape=shapes,
        in_specs=[hbm, hbm] + [vmem] * 5,
        out_specs=[vmem] * 5,
        scratch_shapes=[
            pltpu.VMEM((rows, model), bf16),
            pltpu.VMEM((model, rank), bf16),
            pltpu.VMEM((2, rows, shard), f32),
            pltpu.VMEM((2, rows, shard), f32),
            pltpu.VMEM((2, shard, 2 * rows), bf16),
            pltpu.VMEM((2, width, width), f32),
            pltpu.VMEM((2, width, width), f32),
            pltpu.VMEM((depth - 1, width, width), f32),
            pltpu.VMEM((depth - 1, width, width), f32),
            pltpu.VMEM((2, width // 2, width), f32),
            pltpu.VMEM((2, width, width), f32),
            pltpu.VMEM((2, width // 2, width), f32),
            pltpu.VMEM((rows, rank), f32),
            pltpu.VMEM((rows, rank), f32),
            pltpu.VMEM((2, ushard, rank), f32),
            pltpu.VMEM((2, ushard, rank), f32),
            pltpu.VMEM((features, rank), f32),
            pltpu.VMEM((total, rank), f32),
            pltpu.VMEM((total, rank), f32),
            pltpu.VMEM((total, rank), f32),
            pltpu.VMEM((total // 2, rank), f32),
            pltpu.VMEM((total // 2, rank), f32),
            pltpu.VMEM((total // 4, rank), f32),
            pltpu.VMEM((max(stages - 1, 1), total // 4, rank), f32),
            pltpu.VMEM((max(stages - 1, 1), total // 4, rank), f32),
            dma((2,)), dma((4,)), dma((4,)),
            dma((2 * depth - 2,)), dma((2 * depth - 2,)), dma((2 * depth - 2,)), dma((2 * depth - 2,)),
            dma((2,)), dma((2,)),
            dma((count,)), dma((count,)), dma((count,)), dma((count,)),
            dma((stages, count)), dma((stages, count)),
            dma((count,)), dma((count,)), dma((count,)), dma((count,)),
        ],
        compiler_params=pltpu.CompilerParams(
            collective_id=0, has_side_effects=True
        ),
    )(
        inputs.reshape(rows, model), adapter_down_weight, adapter_up_weight,
        query.reshape(rows, width), key.reshape(rows, width),
        value.reshape(rows, width), output_gradient.reshape(rows, width),
    )
    out = pl.pallas_call(
        write_out,
        out_shape=shapes,
        in_specs=[vmem] * 5,
        out_specs=[hbm] * 5,
        scratch_shapes=[dma((5,))],
    )(*out)
    return tuple(part.reshape(1, rows, width) for part in out[:3]) + tuple(out[3:])


def solution(mesh):
    fused = fits(mesh.shape["seq"], mesh.shape["dp"])
    chosen = fast if fused else local
    return jax.shard_map(
        chosen,
        mesh=mesh,
        in_specs=(
            P("dp", "seq", None),
            P(),
            P(),
            P("dp", "seq", None),
            P("dp", "seq", None),
            P("dp", "seq", None),
            P("dp", "seq", None),
        ),
        out_specs=(
            P("dp", "seq", None),
            P("dp", "seq", None),
            P("dp", "seq", None),
            P("dp", None),
            P("dp", None),
        ),
        check_vma=False,
    )
```
